512 devices in a mesh: occ: 16 (over x_hi, y, core), vir: 32 (over z, x_lo).
Axes of the slice: x: 4 (x_hi: 2, x_lo: 2; x = x_hi * 2 + x_lo), y: 4, z: 16, core: 2. Of those that a mesh axis runs over, the one named last changes fastest.
Arguments:
- orbitals: bfloat16 [16, 8192, 4096], P('occ', 'vir'), may hold values from -0.75 to 0.75
- eps_occ: bfloat16 [16], P('occ'), may hold values from -2.5 to -0.5
- eps_vir: bfloat16 [8192], P('vir'), may hold values from 0.5 to 3
Outputs:
- density: bfloat16 [16, 8192, 4096], P('occ', 'vir')
The draws below stay inside these ranges and needn't reach their ends.
All inputs are finite; a program needn't handle non-finite values.
Results may differ from the reference program's by a relative error of at most 0.0047.
Values may be sent and summed in bfloat16 or wider, within the bound.
No kernel may reach another device: no remote copies, remote signals or barrier semaphores. Data moves between devices by JAX's collectives and lax.ppermute only.
A program may use at most 64 MiB of HBM per device.

```python
import jax
import jax.numpy as jnp
from jax import lax

NAUX = 4096
VIR_DEV = 256
OCC_DEV = 1
BATCH_DEV = 8
REACH = 1
OCC = 16
VIRT = 8192
N_OCC = 16
N_VIR = 32


def shard_levels(own_key, dims, shards, low, largest):
    factor_of, own = 1.0, jax.random.fold_in(own_key, 6)
    for axis_at, shards_of in shards:
        draws = jnp.exp(jax.random.uniform(jax.random.fold_in(own, axis_at), (shards_of,), jnp.float32, low / len(shards), largest / len(shards)))
        factor_of = factor_of * jnp.repeat(draws, dims[axis_at] // shards_of).reshape([-1 if axis == axis_at else 1 for axis in range(len(dims))])
    return factor_of


def centred(own_key, shape, width, bound, split=(), held_as=jnp.bfloat16):
    array = width * jax.random.normal(own_key, shape, jnp.float32)
    if split:
        array = array * shard_levels(own_key, shape, split, -0.22, 0.18)
    return jnp.clip(array, -bound, bound).astype(held_as)


def setup_inputs(seed: int = 0) -> dict:
    arg_keys = jax.random.split(jax.random.key(seed), 4)
    return {
        "orbitals": centred(arg_keys[0], (OCC, VIRT, NAUX), (NAUX ** -0.25), 0.75, ((0, 16), (1, 32))),
        "eps_occ": jnp.clip(-2.5 + 2.0 * jax.random.uniform(arg_keys[1], (OCC,), jnp.float32) ** shard_levels(arg_keys[1], (OCC,), ((0, 16),), -0.2, 0.2), -2.5, -0.5).astype(jnp.bfloat16),
        "eps_vir": jnp.clip(0.5 + 2.5 * jax.random.uniform(arg_keys[2], (VIRT,), jnp.float32) ** shard_levels(arg_keys[2], (VIRT,), ((0, 32),), -0.2, 0.2), 0.5, 3.0).astype(jnp.bfloat16),
    }


def reference(orbitals, eps_occ, eps_vir):
    occ_all, vir_all, aux_width = orbitals.shape
    batch_rows = orbitals.reshape(occ_all, N_VIR, VIR_DEV, aux_width)[:, :, :BATCH_DEV, :]
    batch_rows = batch_rows.reshape(N_OCC, OCC_DEV, N_VIR * BATCH_DEV, aux_width).astype(jnp.float32)
    batch_energy = eps_vir.reshape(N_VIR, VIR_DEV)[:, :BATCH_DEV].reshape(-1).astype(jnp.float32)
    vir_energy = eps_vir.astype(jnp.float32)
    occ_blocks = eps_occ.astype(jnp.float32).reshape(N_OCC, OCC_DEV)
    full = orbitals.reshape(N_OCC, OCC_DEV, vir_all, aux_width)
    offsets = jnp.arange(-REACH, REACH + 1, dtype=jnp.int32)
    highest = lax.Precision.HIGHEST

    def one_block(index):
        partners = ((index + offsets) % N_OCC).astype(jnp.int32)
        resident = full[index].astype(jnp.float32)
        slices = full[partners].astype(jnp.float32)
        row_sets = batch_rows[partners]
        coulomb = jnp.einsum("iap,kjbp->iakjb", resident, row_sets, precision=highest)
        exchange = jnp.einsum("ibp,kjap->iakjb", batch_rows[index], slices, precision=highest)
        denominator = (vir_energy[None, :, None, None, None] + batch_energy[None, None, None, None, :]
                       - occ_blocks[index][:, None, None, None, None]
                       - occ_blocks[partners][None, None, :, :, None])
        amplitude = ((2.0 * coulomb - exchange) / denominator).astype(jnp.bfloat16)
        amplitude = lax.optimization_barrier(amplitude).astype(jnp.float32)
        density = jnp.einsum("iakjb,kjbp->iap", amplitude, row_sets, precision=highest)
        return density.astype(jnp.bfloat16)

    result = lax.map(one_block, jnp.arange(N_OCC, dtype=jnp.int32))
    return result.reshape(occ_all, vir_all, aux_width)
```

```python
import jax
import jax.numpy as jnp
from jax import lax
from jax.experimental import pallas as pl
from jax.experimental.pallas import tpu as pltpu
from jax.sharding import Mesh
from jax.sharding import PartitionSpec as P


BATCH_DEV = 8
CHUNKS = 8
EXTRA = 128

OCC = ("xh", "y", "core")
VIR = ("zq", "zl", "xl")
Z = ("zq", "zl")


def rotate(block, distance):
    size = lax.axis_size(Z)
    return lax.ppermute(block, Z, [((i + distance) % size, i) for i in range(size)])


def pair_up(block):
    size = lax.axis_size(Z)
    return lax.ppermute(block, Z, [((i + 1 if i % 2 else i - 1) % size, i) for i in range(size)])


def swap(block, axis):
    return lax.ppermute(block, axis, [(0, 1), (1, 0)])


def outward(block):
    size = lax.axis_size(OCC)
    route = [((i - 1 if i % 2 == 0 else i + 1) % size, i) for i in range(size)]
    return lax.ppermute(block, OCC, route)


def rows(*blocks):
    return jnp.concatenate(blocks, axis=0)


def contract(a, b):
    return lax.dot_general(a, b, (((1,), (1,)), ((), ())), preferred_element_type=jnp.float32)


def gather_rows(pieces, target, sems, start=0):
    copies, at = [], start
    for n, piece in enumerate(pieces):
        height, width = piece.shape[0], target.shape[1]
        copy = pltpu.make_async_copy(piece.at[:, pl.ds(0, width)], target.at[pl.ds(at, height), :], sems.at[n])
        copy.start()
        copies.append(copy)
        at += height
    return copies


def finish(copies):
    for copy in copies:
        copy.wait()


def own_kernel(vir_ref, x_own, x_mate, x_out, g1, g2, base_ref, a_own_ref, e_mate_ref, e_out_ref, xs, own, tails, sems):
    width = own.shape[1]
    pieces = gather_rows((g1, g2), own, sems)
    for n, (piece, at) in enumerate(((g1, 0), (g2, g1.shape[0]))):
        copy = pltpu.make_async_copy(
            piece.at[:, pl.ds(width, EXTRA)], tails.at[pl.ds(at, piece.shape[0]), :], sems.at[2 + n]
        )
        copy.start()
        pieces.append(copy)
    blocks = [pltpu.make_async_copy(x, xs.at[n], sems.at[4 + n]) for n, x in enumerate((x_own, x_mate, x_out))]
    for copy in blocks:
        copy.start()
    finish(pieces)
    lane = lax.broadcasted_iota(jnp.int32, tails.shape, 1)
    row = lax.broadcasted_iota(jnp.int32, tails.shape, 0)
    tail = tails[...].astype(jnp.float32)
    picked = jnp.where(lane == row % BATCH_DEV, tail, 0.0).astype(jnp.bfloat16)
    batch = contract(jnp.ones((8, EXTRA), jnp.bfloat16), picked)[0:1]
    size = vir_ref.shape[1]
    across = lax.broadcasted_iota(jnp.int32, (size, size), 1) == lax.broadcasted_iota(jnp.int32, (size, size), 0)
    virt = jnp.sum(jnp.where(across, vir_ref[...], 0.0), axis=1, keepdims=True)
    energy = tail[0:1, BATCH_DEV : BATCH_DEV + 1]
    base = virt + batch - energy
    base_ref[...] = base
    blocks[0].wait()
    a_own_ref[...] = (contract(xs[0], own[...]) / (base - energy)).astype(jnp.bfloat16)
    blocks[1].wait()
    e_mate_ref[...] = contract(xs[1], own[...])
    blocks[2].wait()
    e_out_ref[...] = contract(xs[2], own[...])


def pair_amplitude(x_own, block, exchange, base, energy):
    return ((2.0 * contract(x_own, block) - exchange) / (base - energy)).astype(jnp.bfloat16)


def mate_kernel(base_ref, e_mate_ref, tail_ref, x_own, c1, c2, a_mate_ref, xs, mate, sems):
    copies = gather_rows((c1, c2), mate, sems)
    block = pltpu.make_async_copy(x_own, xs, sems.at[2])
    block.start()
    finish(copies)
    block.wait()
    energy = tail_ref[0:1, BATCH_DEV : BATCH_DEV + 1].astype(jnp.float32)
    a_mate_ref[...] = pair_amplitude(xs[...], mate[...], e_mate_ref[...], base_ref[...], energy)


def density_kernel(
    base_ref, e_out_ref, tail_ref, a_own_ref, a_mate_ref, x_own, g1, g2, c1, c2, y1, y2, y3, out_ref, xs, rs, ds, sems
):
    size = base_ref.shape[0]
    out_copies = gather_rows((y1, y2, y3), rs, sems, 2 * size)
    block = pltpu.make_async_copy(x_own, xs, sems.at[3])
    block.start()
    others = gather_rows((g1, g2, c1, c2), rs, sems.at[pl.ds(4, 4)])
    finish(out_copies)
    block.wait()
    energy = tail_ref[0:1, BATCH_DEV : BATCH_DEV + 1].astype(jnp.float32)
    a_out = pair_amplitude(xs[...], rs[pl.ds(2 * size, size), :], e_out_ref[...], base_ref[...], energy)
    finish(others)
    amplitude = jnp.concatenate([a_own_ref[...], a_mate_ref[...], a_out], axis=1)
    stores = []
    for n in range(CHUNKS):
        width = xs.shape[1] // CHUNKS
        at = pl.ds(n * width, width)
        ds[:, at] = jnp.dot(amplitude, rs[:, at], preferred_element_type=jnp.float32).astype(jnp.bfloat16)
        store = pltpu.make_async_copy(ds.at[:, at], out_ref.at[:, at], sems.at[8 + n])
        store.start()
        stores.append(store)
    finish(stores)


def small():
    return pl.BlockSpec(memory_space=pltpu.VMEM)


def large():
    return pl.BlockSpec(memory_space=pl.ANY)


def shards(orbitals, eps_occ, eps_vir):
    x_own = orbitals[0]
    vir_dev, aux = x_own.shape
    x_out = outward(x_own)
    tail = jnp.concatenate([eps_vir[:BATCH_DEV], eps_occ, jnp.zeros(EXTRA - BATCH_DEV - 1, eps_vir.dtype)])
    slab = jnp.concatenate([x_own[:BATCH_DEV], jnp.broadcast_to(tail, (BATCH_DEV, EXTRA))], axis=1)
    n0 = lax.all_gather(slab, "zq", axis=0, tiled=True)
    n0x = swap(n0, "xl")
    up, down = rotate(n0, 1), rotate(n0, -1)
    x_mate = swap(x_own, "core")
    n1 = rows(up, down)
    n1x = swap(n1, "xl")
    even = lax.axis_index("zl") % 2 == 0
    n2 = pair_up(jnp.where(even, up, down))
    g1 = rows(n0, n1, n0x)
    y1 = outward(g1)
    n2x = swap(n2, "xl")
    y2 = outward(rows(n2, n1x))
    g2 = rows(n2, n1x, n2x)
    c1 = swap(g1, "core")
    c2 = swap(g2, "core")
    y3 = outward(n2x)

    batch = g1.shape[0] + g2.shape[0]
    pair_shape = (vir_dev, batch)
    wide = pltpu.VMEM((batch, aux), jnp.bfloat16)
    params = pltpu.CompilerParams(vmem_limit_bytes=24 << 20)
    base, a_own, e_mate, e_out = pl.pallas_call(
        own_kernel,
        out_shape=(
            jax.ShapeDtypeStruct(pair_shape, jnp.float32),
            jax.ShapeDtypeStruct(pair_shape, jnp.bfloat16),
            jax.ShapeDtypeStruct(pair_shape, jnp.float32),
            jax.ShapeDtypeStruct(pair_shape, jnp.float32),
        ),
        in_specs=[small()] + [large()] * 5,
        out_specs=(small(),) * 4,
        scratch_shapes=[
            pltpu.VMEM((3, vir_dev, aux), jnp.bfloat16),
            wide,
            pltpu.VMEM((batch, EXTRA), jnp.bfloat16),
            pltpu.SemaphoreType.DMA((7,)),
        ],
        compiler_params=params,
    )(eps_vir.astype(jnp.float32)[None], x_own, x_mate, x_out, g1, g2)
    a_mate = pl.pallas_call(
        mate_kernel,
        out_shape=jax.ShapeDtypeStruct(pair_shape, jnp.bfloat16),
        in_specs=[small()] * 3 + [large()] * 3,
        out_specs=small(),
        scratch_shapes=[pltpu.VMEM((vir_dev, aux), jnp.bfloat16), wide, pltpu.SemaphoreType.DMA((3,))],
        compiler_params=params,
    )(base, e_mate, c1[:BATCH_DEV, aux:], x_own, c1, c2)
    density = pl.pallas_call(
        density_kernel,
        out_shape=jax.ShapeDtypeStruct((vir_dev, aux), jnp.bfloat16),
        in_specs=[small()] * 5 + [large()] * 8,
        out_specs=large(),
        scratch_shapes=[
            pltpu.VMEM((vir_dev, aux), jnp.bfloat16),
            pltpu.VMEM((3 * batch, aux), jnp.bfloat16),
            pltpu.VMEM((vir_dev, aux), jnp.bfloat16),
            pltpu.SemaphoreType.DMA((8 + CHUNKS,)),
        ],
        compiler_params=params,
    )(base, e_out, y1[:BATCH_DEV, aux:], a_own, a_mate, x_own, g1, g2, c1, c2, y1, y2, y3)
    return density[None]


def solution(mesh):
    fine = Mesh(mesh.devices.reshape(2, 4, 2, 4, 4, 2), OCC + VIR)

    return jax.shard_map(
        shards,
        mesh=fine,
        in_specs=(P(OCC, VIR, None), P(OCC), P(VIR)),
        out_specs=P(OCC, VIR, None),
        check_vma=False,
    )
```

```python
import jax
import jax.numpy as jnp
from jax import lax
from jax.experimental import pallas as pl
from jax.experimental.pallas import tpu as pltpu
from jax.sharding import Mesh
from jax.sharding import PartitionSpec as P


BATCH_DEV = 8
CHUNKS = 8
EXTRA = 128

OCC = ("xh", "y", "core")
VIR = ("zq", "zl", "xl")
Z = ("zq", "zl")


def rotate(block, distance):
    size = lax.axis_size(Z)
    return lax.ppermute(block, Z, [((i + distance) % size, i) for i in range(size)])


def pair_up(block):
    size = lax.axis_size(Z)
    return lax.ppermute(block, Z, [((i + 1 if i % 2 else i - 1) % size, i) for i in range(size)])


def swap(block, axis):
    return lax.ppermute(block, axis, [(0, 1), (1, 0)])


def outward(block):
    size = lax.axis_size(OCC)
    route = [((i - 1 if i % 2 == 0 else i + 1) % size, i) for i in range(size)]
    return lax.ppermute(block, OCC, route)


def rows(*blocks):
    return jnp.concatenate(blocks, axis=0)


def contract(a, b):
    return lax.dot_general(a, b, (((1,), (1,)), ((), ())), preferred_element_type=jnp.float32)


def gather_rows(pieces, target, sems, start=0):
    copies, at = [], start
    for n, piece in enumerate(pieces):
        height, width = piece.shape[0], target.shape[1]
        copy = pltpu.make_async_copy(piece.at[:, pl.ds(0, width)], target.at[pl.ds(at, height), :], sems.at[n])
        copy.start()
        copies.append(copy)
        at += height
    return copies


def finish(copies):
    for copy in copies:
        copy.wait()


def own_kernel(vir_ref, x_own, x_mate, x_out, p1, p2, p3, base_ref, a_own_ref, e_mate_ref, e_out_ref, xs, own, tails, sems):
    width = own.shape[1]
    pieces = gather_rows((p1, p2, p3), own, sems)
    at = 0
    for n, piece in enumerate((p1, p2, p3)):
        copy = pltpu.make_async_copy(
            piece.at[:, pl.ds(width, EXTRA)], tails.at[pl.ds(at, piece.shape[0]), :], sems.at[3 + n]
        )
        copy.start()
        pieces.append(copy)
        at += piece.shape[0]
    blocks = [pltpu.make_async_copy(x, xs.at[n], sems.at[6 + n]) for n, x in enumerate((x_own, x_mate, x_out))]
    for copy in blocks:
        copy.start()
    finish(pieces)
    lane = lax.broadcasted_iota(jnp.int32, tails.shape, 1)
    row = lax.broadcasted_iota(jnp.int32, tails.shape, 0)
    tail = tails[...].astype(jnp.float32)
    picked = jnp.where(lane == row % BATCH_DEV, tail, 0.0).astype(jnp.bfloat16)
    batch = contract(jnp.ones((8, EXTRA), jnp.bfloat16), picked)[0:1]
    size = vir_ref.shape[1]
    across = lax.broadcasted_iota(jnp.int32, (size, size), 1) == lax.broadcasted_iota(jnp.int32, (size, size), 0)
    virt = jnp.sum(jnp.where(across, vir_ref[...], 0.0), axis=1, keepdims=True)
    energy = tail[0:1, BATCH_DEV : BATCH_DEV + 1]
    base = virt + batch - energy
    base_ref[...] = base
    blocks[0].wait()
    a_own_ref[...] = (contract(xs[0], own[...]) / (base - energy)).astype(jnp.bfloat16)
    blocks[1].wait()
    e_mate_ref[...] = contract(xs[1], own[...])
    blocks[2].wait()
    e_out_ref[...] = contract(xs[2], own[...])


def pair_amplitude(x_own, block, exchange, base, energy):
    return ((2.0 * contract(x_own, block) - exchange) / (base - energy)).astype(jnp.bfloat16)


def mate_kernel(base_ref, e_mate_ref, tail_ref, x_own, c1, c2, c3, a_mate_ref, xs, mate, sems):
    copies = gather_rows((c1, c2, c3), mate, sems)
    block = pltpu.make_async_copy(x_own, xs, sems.at[3])
    block.start()
    finish(copies)
    block.wait()
    energy = tail_ref[0:1, BATCH_DEV : BATCH_DEV + 1].astype(jnp.float32)
    a_mate_ref[...] = pair_amplitude(xs[...], mate[...], e_mate_ref[...], base_ref[...], energy)


def density_kernel(base_ref, e_out_ref, tail_ref, a_own_ref, a_mate_ref, x_own, *refs):
    *pieces, out_ref, xs, rs, ds, sems = refs
    size = base_ref.shape[0]
    out_copies = gather_rows(pieces[6:], rs, sems, 2 * size)
    block = pltpu.make_async_copy(x_own, xs, sems.at[3])
    block.start()
    others = gather_rows(pieces[:6], rs, sems.at[pl.ds(4, 6)])
    finish(out_copies)
    block.wait()
    energy = tail_ref[0:1, BATCH_DEV : BATCH_DEV + 1].astype(jnp.float32)
    a_out = pair_amplitude(xs[...], rs[pl.ds(2 * size, size), :], e_out_ref[...], base_ref[...], energy)
    finish(others)
    amplitude = jnp.concatenate([a_own_ref[...], a_mate_ref[...], a_out], axis=1)
    stores = []
    for n in range(CHUNKS):
        width = xs.shape[1] // CHUNKS
        at = pl.ds(n * width, width)
        ds[:, at] = jnp.dot(amplitude, rs[:, at], preferred_element_type=jnp.float32).astype(jnp.bfloat16)
        store = pltpu.make_async_copy(ds.at[:, at], out_ref.at[:, at], sems.at[10 + n])
        store.start()
        stores.append(store)
    finish(stores)


def small():
    return pl.BlockSpec(memory_space=pltpu.VMEM)


def large():
    return pl.BlockSpec(memory_space=pl.ANY)


def shards(orbitals, eps_occ, eps_vir):
    x_own = orbitals[0]
    vir_dev, aux = x_own.shape
    x_out = outward(x_own)
    tail = jnp.concatenate([eps_vir[:BATCH_DEV], eps_occ, jnp.zeros(EXTRA - BATCH_DEV - 1, eps_vir.dtype)])
    slab = jnp.concatenate([x_own[:BATCH_DEV], jnp.broadcast_to(tail, (BATCH_DEV, EXTRA))], axis=1)
    part = lax.all_gather(slab, "zq", axis=0, tiled=True)
    first = rows(part, swap(part, "xl"))
    up, down = rotate(first, 1), rotate(first, -1)
    x_mate = swap(x_own, "core")
    y1 = outward(first)
    c1 = swap(first, "core")
    even = lax.axis_index("zl") % 2 == 0
    third = pair_up(jnp.where(even, up, down))
    second = rows(up, down)
    y2 = outward(second)
    c2 = swap(second, "core")
    y3 = outward(third)
    c3 = swap(third, "core")
    own, mate, out = (first, second, third), (c1, c2, c3), (y1, y2, y3)

    batch = sum(piece.shape[0] for piece in own)
    pair_shape = (vir_dev, batch)
    wide = pltpu.VMEM((batch, aux), jnp.bfloat16)
    params = pltpu.CompilerParams(vmem_limit_bytes=24 << 20)
    base, a_own, e_mate, e_out = pl.pallas_call(
        own_kernel,
        out_shape=(
            jax.ShapeDtypeStruct(pair_shape, jnp.float32),
            jax.ShapeDtypeStruct(pair_shape, jnp.bfloat16),
            jax.ShapeDtypeStruct(pair_shape, jnp.float32),
            jax.ShapeDtypeStruct(pair_shape, jnp.float32),
        ),
        in_specs=[small()] + [large()] * 6,
        out_specs=(small(),) * 4,
        scratch_shapes=[
            pltpu.VMEM((3, vir_dev, aux), jnp.bfloat16),
            wide,
            pltpu.VMEM((batch, EXTRA), jnp.bfloat16),
            pltpu.SemaphoreType.DMA((9,)),
        ],
        compiler_params=params,
    )(eps_vir.astype(jnp.float32)[None], x_own, x_mate, x_out, *own)
    a_mate = pl.pallas_call(
        mate_kernel,
        out_shape=jax.ShapeDtypeStruct(pair_shape, jnp.bfloat16),
        in_specs=[small()] * 3 + [large()] * 4,
        out_specs=small(),
        scratch_shapes=[pltpu.VMEM((vir_dev, aux), jnp.bfloat16), wide, pltpu.SemaphoreType.DMA((4,))],
        compiler_params=params,
    )(base, e_mate, c1[:BATCH_DEV, aux:], x_own, *mate)
    density = pl.pallas_call(
        density_kernel,
        out_shape=jax.ShapeDtypeStruct((vir_dev, aux), jnp.bfloat16),
        in_specs=[small()] * 5 + [large()] * 10,
        out_specs=large(),
        scratch_shapes=[
            pltpu.VMEM((vir_dev, aux), jnp.bfloat16),
            pltpu.VMEM((3 * batch, aux), jnp.bfloat16),
            pltpu.VMEM((vir_dev, aux), jnp.bfloat16),
            pltpu.SemaphoreType.DMA((10 + CHUNKS,)),
        ],
        compiler_params=params,
    )(base, e_out, y1[:BATCH_DEV, aux:], a_own, a_mate, x_own, *own, *mate, *out)
    return density[None]


def solution(mesh):
    fine = Mesh(mesh.devices.reshape(2, 4, 2, 4, 4, 2), OCC + VIR)

    return jax.shard_map(
        shards,
        mesh=fine,
        in_specs=(P(OCC, VIR, None), P(OCC), P(VIR)),
        out_specs=P(OCC, VIR, None),
        check_vma=False,
    )
```

```python
import jax
import jax.numpy as jnp
from jax import lax
from jax.experimental import pallas as pl
from jax.experimental.pallas import tpu as pltpu
from jax.sharding import Mesh
from jax.sharding import PartitionSpec as P


BATCH_DEV = 8
CHUNKS = 8
EXTRA = 128

OCC = ("xh", "y", "core")
VIR = ("zq", "zl", "xl")
Z = ("zq", "zl")


def rotate(block, distance):
    size = lax.axis_size(Z)
    return lax.ppermute(block, Z, [((i + distance) % size, i) for i in range(size)])


def pair_up(block):
    size = lax.axis_size(Z)
    return lax.ppermute(block, Z, [((i + 1 if i % 2 else i - 1) % size, i) for i in range(size)])


def swap(block, axis):
    return lax.ppermute(block, axis, [(0, 1), (1, 0)])


def outward(block):
    size = lax.axis_size(OCC)
    route = [((i - 1 if i % 2 == 0 else i + 1) % size, i) for i in range(size)]
    return lax.ppermute(block, OCC, route)


def rows(*blocks):
    return jnp.concatenate(blocks, axis=0)


def contract(a, b):
    return lax.dot_general(a, b, (((1,), (1,)), ((), ())), preferred_element_type=jnp.float32)


def gather_rows(pieces, target, sems, start=0):
    copies, at = [], start
    for n, piece in enumerate(pieces):
        height, width = piece.shape[0], target.shape[1]
        copy = pltpu.make_async_copy(piece.at[:, pl.ds(0, width)], target.at[pl.ds(at, height), :], sems.at[n])
        copy.start()
        copies.append(copy)
        at += height
    return copies


def finish(copies):
    for copy in copies:
        copy.wait()


def own_kernel(vir_ref, x_own, x_mate, x_out, rows_own, base_ref, a_own_ref, e_mate_ref, e_out_ref, xs, own, tails, sems):
    width = own.shape[1]
    pieces = gather_rows((rows_own,), own, sems)
    pieces.append(pltpu.make_async_copy(rows_own.at[:, pl.ds(width, EXTRA)], tails, sems.at[1]))
    pieces[1].start()
    blocks = [pltpu.make_async_copy(x, xs.at[n], sems.at[2 + n]) for n, x in enumerate((x_own, x_mate, x_out))]
    for copy in blocks:
        copy.start()
    finish(pieces)
    lane = lax.broadcasted_iota(jnp.int32, tails.shape, 1)
    row = lax.broadcasted_iota(jnp.int32, tails.shape, 0)
    tail = tails[...].astype(jnp.float32)
    picked = jnp.where(lane == row % BATCH_DEV, tail, 0.0).astype(jnp.bfloat16)
    batch = contract(jnp.ones((8, EXTRA), jnp.bfloat16), picked)[0:1]
    size = vir_ref.shape[1]
    across = lax.broadcasted_iota(jnp.int32, (size, size), 1) == lax.broadcasted_iota(jnp.int32, (size, size), 0)
    virt = jnp.sum(jnp.where(across, vir_ref[...], 0.0), axis=1, keepdims=True)
    energy = tail[0:1, BATCH_DEV : BATCH_DEV + 1]
    base = virt + batch - energy
    base_ref[...] = base
    blocks[0].wait()
    a_own_ref[...] = (contract(xs[0], own[...]) / (base - energy)).astype(jnp.bfloat16)
    blocks[1].wait()
    e_mate_ref[...] = contract(xs[1], own[...])
    blocks[2].wait()
    e_out_ref[...] = contract(xs[2], own[...])


def pair_amplitude(x_own, block, exchange, base, energy):
    return ((2.0 * contract(x_own, block) - exchange) / (base - energy)).astype(jnp.bfloat16)


def mate_kernel(base_ref, e_mate_ref, tail_ref, x_own, rows_mate, a_mate_ref, xs, mate, sems):
    copies = gather_rows((rows_mate,), mate, sems)
    block = pltpu.make_async_copy(x_own, xs, sems.at[1])
    block.start()
    finish(copies)
    block.wait()
    energy = tail_ref[0:1, BATCH_DEV : BATCH_DEV + 1].astype(jnp.float32)
    a_mate_ref[...] = pair_amplitude(xs[...], mate[...], e_mate_ref[...], base_ref[...], energy)


def density_kernel(base_ref, e_out_ref, tail_ref, a_own_ref, a_mate_ref, x_own, *refs):
    *pieces, out_ref, xs, rs, ds, sems = refs
    size = base_ref.shape[0]
    out_copies = gather_rows(pieces[2:], rs, sems, 2 * size)
    block = pltpu.make_async_copy(x_own, xs, sems.at[3])
    block.start()
    others = gather_rows(pieces[:2], rs, sems.at[pl.ds(4, 2)])
    finish(out_copies)
    block.wait()
    energy = tail_ref[0:1, BATCH_DEV : BATCH_DEV + 1].astype(jnp.float32)
    a_out = pair_amplitude(xs[...], rs[pl.ds(2 * size, size), :], e_out_ref[...], base_ref[...], energy)
    finish(others)
    amplitude = jnp.concatenate([a_own_ref[...], a_mate_ref[...], a_out], axis=1)
    stores = []
    for n in range(CHUNKS):
        width = xs.shape[1] // CHUNKS
        at = pl.ds(n * width, width)
        ds[:, at] = jnp.dot(amplitude, rs[:, at], preferred_element_type=jnp.float32).astype(jnp.bfloat16)
        store = pltpu.make_async_copy(ds.at[:, at], out_ref.at[:, at], sems.at[6 + n])
        store.start()
        stores.append(store)
    finish(stores)


def small():
    return pl.BlockSpec(memory_space=pltpu.VMEM)


def large():
    return pl.BlockSpec(memory_space=pl.ANY)


def shards(orbitals, eps_occ, eps_vir):
    x_own = orbitals[0]
    vir_dev, aux = x_own.shape
    x_out = outward(x_own)
    tail = jnp.concatenate([eps_vir[:BATCH_DEV], eps_occ, jnp.zeros(EXTRA - BATCH_DEV - 1, eps_vir.dtype)])
    slab = jnp.concatenate([x_own[:BATCH_DEV], jnp.broadcast_to(tail, (BATCH_DEV, EXTRA))], axis=1)
    part = lax.all_gather(slab, "zq", axis=0, tiled=True)
    part_x = swap(part, "xl")
    even = lax.axis_index("zl") % 2 == 0
    up, down = rotate(part, 1), rotate(part, -1)
    up_x, down_x = rotate(part_x, 1), rotate(part_x, -1)
    x_mate = swap(x_own, "core")
    y1 = outward(rows(part, part_x))
    two = pair_up(jnp.where(even, up, down))
    y2 = outward(rows(up, down, up_x, down_x))
    two_x = pair_up(jnp.where(even, up_x, down_x))
    y3 = outward(rows(two, two_x))
    own = rows(part, part_x, up, down, up_x, down_x, two, two_x)
    mate = swap(own, "core")
    out = (y1, y2, y3)

    batch = own.shape[0]
    pair_shape = (vir_dev, batch)
    wide = pltpu.VMEM((batch, aux), jnp.bfloat16)
    params = pltpu.CompilerParams(vmem_limit_bytes=24 << 20)
    base, a_own, e_mate, e_out = pl.pallas_call(
        own_kernel,
        out_shape=(
            jax.ShapeDtypeStruct(pair_shape, jnp.float32),
            jax.ShapeDtypeStruct(pair_shape, jnp.bfloat16),
            jax.ShapeDtypeStruct(pair_shape, jnp.float32),
            jax.ShapeDtypeStruct(pair_shape, jnp.float32),
        ),
        in_specs=[small()] + [large()] * 4,
        out_specs=(small(),) * 4,
        scratch_shapes=[
            pltpu.VMEM((3, vir_dev, aux), jnp.bfloat16),
            wide,
            pltpu.VMEM((batch, EXTRA), jnp.bfloat16),
            pltpu.SemaphoreType.DMA((5,)),
        ],
        compiler_params=params,
    )(eps_vir.astype(jnp.float32)[None], x_own, x_mate, x_out, own)
    a_mate = pl.pallas_call(
        mate_kernel,
        out_shape=jax.ShapeDtypeStruct(pair_shape, jnp.bfloat16),
        in_specs=[small()] * 3 + [large()] * 2,
        out_specs=small(),
        scratch_shapes=[pltpu.VMEM((vir_dev, aux), jnp.bfloat16), wide, pltpu.SemaphoreType.DMA((2,))],
        compiler_params=params,
    )(base, e_mate, mate[:BATCH_DEV, aux:], x_own, mate)
    density = pl.pallas_call(
        density_kernel,
        out_shape=jax.ShapeDtypeStruct((vir_dev, aux), jnp.bfloat16),
        in_specs=[small()] * 5 + [large()] * 6,
        out_specs=large(),
        scratch_shapes=[
            pltpu.VMEM((vir_dev, aux), jnp.bfloat16),
            pltpu.VMEM((3 * batch, aux), jnp.bfloat16),
            pltpu.VMEM((vir_dev, aux), jnp.bfloat16),
            pltpu.SemaphoreType.DMA((6 + CHUNKS,)),
        ],
        compiler_params=params,
    )(base, e_out, y1[:BATCH_DEV, aux:], a_own, a_mate, x_own, own, mate, *out)
    return density[None]


def solution(mesh):
    fine = Mesh(mesh.devices.reshape(2, 4, 2, 4, 4, 2), OCC + VIR)

    return jax.shard_map(
        shards,
        mesh=fine,
        in_specs=(P(OCC, VIR, None), P(OCC), P(VIR)),
        out_specs=P(OCC, VIR, None),
        check_vma=False,
    )
```
